512 devices in a mesh: pair: 128 (over x, z, core), sect: 4 (over y).
Axes of the slice: x: 4, y: 4, z: 16, core: 2. Of those that a mesh axis runs over, the one named last changes fastest.
Arguments:
- operators: float32 [256, 1024, 1024], P('pair', 'sect'), may hold values from -6 to 6
- rotations: float32 [128, 1024, 768], P('pair', 'sect'), may hold values from -0.1875 to 0.1875
- sector_owner: int32 [1], replicated, may hold values from 0 to 127
- slot_pair: int32 [256], replicated, may hold values from 0 to 255, each once
- sources: int32 [256, 16], replicated, may hold values from 0 to 255
- integrals: float32 [256, 16], replicated, may hold values from -3 to 3
- term_count: int32 [256], replicated, may hold values from 1 to 16, 1024 in all
Outputs:
- complement: float32 [256, 768, 768], P('pair', 'sect')
The draws below stay inside these ranges and needn't reach their ends.
Inputs may be any that keep to these rules, and one draw needn't show every extreme that they name: `sector_owner`: a pair index along the pair axis. `slot_pair`: each orbital-pair id appears once. `sources`: ids may repeat within a list. `term_count`: the counts sum to 1024 and the largest is exactly 16.
All inputs are finite; a program needn't handle non-finite values.
Results may differ from the reference program's by a relative error of at most 0.0001.
Values sent between devices are 32-bit elements; how exact they have to be, the bound alone decides.
No kernel may reach another device: no remote copies, remote signals or barrier semaphores. Data moves between devices by JAX's collectives and lax.ppermute only.
A program may use at most 64 MiB of HBM per device.

```python
import math
import jax
import jax.numpy as jnp
import numpy as np
from jax import lax

M = 1024
MNEW = 768
R = 16
N_OPS = 256
N_PAIR = 128


def touch_ends(result, stream_key, least, high):
    longest = result.shape.index(max(result.shape))
    spots = []
    for shift in (0, 1):
        where = [jax.random.randint(jax.random.fold_in(stream_key, axis), (), 0, length) for axis, length in enumerate(result.shape)]
        where[longest] = (where[longest] + shift) % result.shape[longest]
        spots.append(tuple(where))
    return result.at[spots[0]].set(least).at[spots[1]].set(high)


def steps_of(stream_key, extent, shards, low, largest):
    loudness, own = 1.0, jax.random.fold_in(stream_key, 6)
    for position, shards_of in shards:
        heights = jnp.exp(jax.random.uniform(jax.random.fold_in(own, position), (shards_of,), jnp.float32, low / len(shards), largest / len(shards)))
        loudness = loudness * jnp.repeat(heights, extent[position] // shards_of).reshape([-1 if axis == position else 1 for axis in range(len(extent))])
    return loudness


def profile(amount, total, bound, skew):
    portions = [(1 << 20) // math.isqrt(standing ** skew) + 1 for standing in range(2, amount + 1)]
    rest, holding = total - bound - (amount - 1), [1] * (amount - 1)
    while rest > 0:
        candidates = [i for i in range(amount - 1) if holding[i] < bound]
        whole, remaining = sum([portions[i] for i in candidates]), rest
        for i in candidates:
            extra = min(bound - holding[i], max(1, remaining * portions[i] // whole), rest)
            holding[i] = holding[i] + extra
            rest = rest - extra
    return np.array([bound] + holding)


def uneven_parts(key, count, total, limit, slope):
    if count == 2:
        one = jax.random.randint(key, (), max(1, total - limit), min(limit, total - 1) + 1)
        return jnp.stack([one, total - one])
    tallies = jnp.asarray(profile(count, total, limit, slope), jnp.int32)
    pairs = (count - 1) // 2
    donor, sink = tallies[1:1 + 2 * pairs:2], tallies[2:2 + 2 * pairs:2]
    room = jnp.minimum(donor - 1, limit - sink)
    passed = jax.random.randint(jax.random.fold_in(key, 1), (pairs,), 0, 1 << 20) % (room + 1)
    tallies = tallies.at[1:1 + 2 * pairs:2].set(donor - passed).at[2:2 + 2 * pairs:2].set(sink + passed)
    return tallies[jax.random.permutation(jax.random.fold_in(key, 2), count)]


def gaussian(own_key, extent, spread, limit, split=(), kind=jnp.bfloat16):
    entries = jax.random.normal(own_key, extent, jnp.float32) * spread
    if len(split) > 0:
        entries = steps_of(own_key, extent, split, -0.22, 0.18) * entries
    return jnp.clip(entries, min=-limit, max=limit).astype(kind)


def setup_inputs(seed: int = 0) -> dict:
    arg_keys = jax.random.split(jax.random.key(seed), 8)
    return {
        "operators": gaussian(arg_keys[0], (N_OPS, M, M), 1.0, 6.0, ((0, 128), (1, 4)), jnp.float32),
        "rotations": gaussian(arg_keys[1], (N_PAIR, M, MNEW), M ** -0.5, 0.1875, ((0, 128), (1, 4)), jnp.float32),
        "sector_owner": jax.random.randint(arg_keys[2], (1,), 0, N_PAIR).astype(jnp.int32),
        "slot_pair": jax.random.permutation(arg_keys[3], N_OPS).astype(jnp.int32),
        "sources": touch_ends(jax.random.randint(arg_keys[4], (N_OPS, R), 0, N_OPS), jax.random.fold_in(arg_keys[4], 1), 0, N_OPS - 1).astype(jnp.int32),
        "integrals": gaussian(arg_keys[5], (N_OPS, R), 0.5, 3.0, (), jnp.float32),
        "term_count": uneven_parts(arg_keys[6], N_OPS, 4 * N_OPS, R, 2).astype(jnp.int32),
    }


def coupling_matrix(slot_pair, sources, integrals, term_count):
    is_live = lax.broadcasted_iota(jnp.int32, sources.shape, 1) < term_count[:, None]
    weighted = jnp.where(is_live, integrals, jnp.zeros_like(integrals))
    matches = (sources[:, :, None] == slot_pair[None, None, :]).astype(integrals.dtype)
    return jnp.sum(weighted[:, :, None] * matches, axis=1)


def reference(operators, rotations, sector_owner, slot_pair, sources, integrals, term_count):
    rotation = lax.dynamic_index_in_dim(rotations, sector_owner[0], 0, keepdims=False)

    def renormalize(operator):
        half_done = jnp.dot(operator, rotation, precision=lax.Precision.HIGHEST, preferred_element_type=jnp.float32)
        return jnp.dot(rotation.T, half_done, precision=lax.Precision.HIGHEST, preferred_element_type=jnp.float32)

    renormalized = lax.map(renormalize, operators)
    coupling = coupling_matrix(slot_pair, sources, integrals, term_count)
    flattened = renormalized.reshape(renormalized.shape[0], -1)
    mixture = jnp.dot(coupling, flattened, precision=lax.Precision.HIGHEST, preferred_element_type=jnp.float32)
    return mixture.reshape(renormalized.shape)
```

```python
import jax
import jax.numpy as jnp
from jax import lax
from jax.experimental import pallas as pl
from jax.experimental.pallas import tpu as pltpu
from jax.sharding import Mesh, PartitionSpec as P


NX, NZ, NC, NY = 4, 16, 2, 4
N_PAIR = NX * NZ * NC
PAIR = ("x", "z", "c")
LANES = 128
F32, BF16 = jnp.float32, jnp.bfloat16


def exchange(chunks, axes):
    return lax.all_to_all(chunks, axes, split_axis=0, concat_axis=0, tiled=True)


def gather(piece, axes, count):
    return exchange(jnp.broadcast_to(piece, (count, *piece.shape)), axes)


def two_parts(value):
    high = value.astype(BF16)
    return high, (value - high.astype(F32)).astype(BF16)


def dot3(left, right, dims):
    (lh, ll), (rh, rl) = left, right

    def one(a, b):
        return lax.dot_general(a, b, (dims, ((), ())), preferred_element_type=F32)

    return one(lh, rh) + (one(lh, rl) + one(ll, rh))


def spread_rotation(slab, owner):
    x_own, z_own, c_own = owner // (NZ * NC), (owner // NC) % NZ, owner % NC
    flipped = slab.T
    new, few = flipped.shape
    rows = new // (NC * NX)
    piece = exchange(flipped.reshape(NC * NX, rows, few), ("c", "x"))
    piece = lax.dynamic_index_in_dim(piece, c_own * NX + x_own, 0, keepdims=False)
    piece = exchange(piece.reshape(NZ, rows // NZ, few), "z")
    piece = lax.dynamic_index_in_dim(piece, z_own, 0, keepdims=False)
    piece = gather(piece, "z", NZ).reshape(rows, few)
    piece = gather(piece, ("y", "x"), NY * NX)
    return piece.reshape(NY, NX * rows, few)


def split_columns(operators, y):
    n_ops, few, old = operators.shape
    cols = old // NY

    def body(y_ref, *refs):
        for source, target in zip(refs[:NY], refs[NY:], strict=True):
            target[...] = source[0]

    return pl.pallas_call(
        body,
        grid_spec=pltpu.PrefetchScalarGridSpec(
            num_scalar_prefetch=1,
            grid=(n_ops,),
            in_specs=[
                pl.BlockSpec((1, few, cols), lambda g, y_ref, hop=hop: (g, 0, lax.rem(y_ref[0] + hop, NY)))
                for hop in range(NY)
            ],
            out_specs=[pl.BlockSpec((few, cols), lambda g, y_ref: (0, g))] * NY,
        ),
        out_shape=[jax.ShapeDtypeStruct((few, n_ops * cols), F32)] * NY,
        cost_estimate=pl.CostEstimate(flops=0, bytes_accessed=8 * operators.size, transcendentals=0),
        name="split_columns",
    )(y, *[operators] * NY)


def multiply_left(place, half, blocks, before=None):
    n_half, few = half.shape[1:]
    wide = blocks[0].shape[1]
    rows = NY * n_half // 2 // NY

    def body(place_ref, half_ref, *refs):
        block_refs, refs = refs[:NY], refs[NY:]
        out_ref, th, tl, oh, ol = refs[-5:]
        for hop in range(NY):
            part = pl.ds(hop * few, few)
            th[:, part], tl[:, part] = two_parts(half_ref[lax.rem(place_ref[0] + NY - hop, NY)])
            oh[part, :], ol[part, :] = two_parts(block_refs[hop][...])
        done = dot3((th[...], tl[...]), (oh[...], ol[...]), ((1,), (0,)))
        for q in range(2):
            out_ref[q] = done[q * rows : (q + 1) * rows]

    whole = lambda *shape: pl.BlockSpec(shape, lambda i, place_ref: (0,) * len(shape))
    extra = [] if before is None else [before]
    return pl.pallas_call(
        body,
        grid_spec=pltpu.PrefetchScalarGridSpec(
            num_scalar_prefetch=1,
            grid=(1,),
            in_specs=[whole(*half.shape)]
            + [whole(*b.shape) for b in blocks]
            + [pl.BlockSpec(memory_space=pl.ANY)] * len(extra),
            out_specs=pl.BlockSpec((2, rows, wide), lambda i, place_ref: (place_ref[1], 0, 0)),
            scratch_shapes=[
                pltpu.VMEM((n_half, NY * few), BF16),
                pltpu.VMEM((n_half, NY * few), BF16),
                pltpu.VMEM((NY * few, wide), BF16),
                pltpu.VMEM((NY * few, wide), BF16),
            ],
        ),
        out_shape=jax.ShapeDtypeStruct((4, rows, wide), F32),
        input_output_aliases={} if before is None else {2 + NY: 0},
        cost_estimate=pl.CostEstimate(
            flops=6 * n_half * NY * few * wide, bytes_accessed=4 * half.size + 20 * blocks[0].size, transcendentals=0
        ),
        name="multiply_left",
    )(place, half, *blocks, *extra)


def multiply_right(core, by_row, own, other):
    rows = by_row.shape[1]
    n_half, few = own.shape[1:]
    n_ops = by_row.shape[2] // few
    triples, strips = rows // 3, n_half // LANES
    per = n_ops * 3 * strips

    def body(core_ref, row_ref, own_ref, other_ref, out_ref, rh, rl, th, tl, z):
        for s in range(NY):
            part = pl.ds(s * few, few)
            for g in range(n_ops):
                band = pl.ds(g * rows, rows)
                rh[band, part], rl[band, part] = two_parts(row_ref[s, :, g * few : (g + 1) * few])
        for turn, ref in enumerate((own_ref, other_ref)):
            for s in range(NY):
                part = pl.ds(s * few, few)
                th[:, part], tl[:, part] = two_parts(ref[s])
            done = dot3((rh[...], rl[...]), (th[...], tl[...]), ((1,), (1,)))
            side = core_ref[0] if turn == 0 else 1 - core_ref[0]
            for strip in range(strips):
                z[strip] = done[:, strip * LANES : (strip + 1) * LANES]
            for g in range(n_ops):
                for r in range(3):
                    for strip in range(strips):
                        at = g * 3 * strips + r * strips + strip
                        out_ref[side, pl.ds(at, triples, stride=per), :] = z[
                            strip, pl.ds(g * rows + r, triples, stride=3), :
                        ]

    whole = lambda *shape: pl.BlockSpec(shape, lambda i, core_ref: (0,) * len(shape))
    out = (2, triples * per, LANES)
    return pl.pallas_call(
        body,
        grid_spec=pltpu.PrefetchScalarGridSpec(
            num_scalar_prefetch=1,
            grid=(1,),
            in_specs=[whole(*by_row.shape), whole(*own.shape), whole(*other.shape)],
            out_specs=whole(*out),
            scratch_shapes=[
                pltpu.VMEM((n_ops * rows, NY * few), BF16),
                pltpu.VMEM((n_ops * rows, NY * few), BF16),
                pltpu.VMEM((n_half, NY * few), BF16),
                pltpu.VMEM((n_half, NY * few), BF16),
                pltpu.VMEM((strips, n_ops * rows, LANES), F32),
            ],
        ),
        out_shape=jax.ShapeDtypeStruct(out, F32),
        cost_estimate=pl.CostEstimate(
            flops=12 * n_ops * rows * NY * few * n_half, bytes_accessed=16 * own.size, transcendentals=0
        ),
        name="multiply_right",
    )(core, by_row, own, other)


def mix(coupling, spread):
    n_all = coupling.shape[0]
    n_ops = n_all // N_PAIR
    per = spread.shape[0] // N_PAIR
    strips = per // n_ops

    def body(c_ref, x_ref, out_ref, xh, xl):
        for g in range(n_ops):
            for k in range(strips):
                part = x_ref[pl.ds(g * strips + k, N_PAIR, stride=per), :]
                at = (pl.ds(g * N_PAIR, N_PAIR), pl.ds(k * LANES, LANES))
                xh[at], xl[at] = two_parts(part)
        done = dot3(two_parts(c_ref[...]), (xh[...], xl[...]), ((1,), (0,)))
        for g in range(n_ops):
            for k in range(strips):
                out_ref[pl.ds(g * strips + k, N_PAIR, stride=per), :] = done[
                    g * N_PAIR : (g + 1) * N_PAIR, k * LANES : (k + 1) * LANES
                ]

    return pl.pallas_call(
        body,
        out_shape=jax.ShapeDtypeStruct(spread.shape, F32),
        scratch_shapes=[pltpu.VMEM((n_all, strips * LANES), BF16)] * 2,
        cost_estimate=pl.CostEstimate(
            flops=6 * n_all * n_all * strips * LANES, bytes_accessed=8 * spread.size, transcendentals=0
        ),
        name="mix",
    )(coupling, spread)


def place_rows(back, rows, width):
    triples = rows // 3
    strips = width // 2 // LANES
    per = back.shape[0] // (2 * triples)
    n_ops = per // (3 * strips)

    def body(in_ref, out_ref, band):
        for g in range(n_ops):
            for h in range(2):
                for strip in range(strips):
                    for r in range(3):
                        at = h * triples * per + g * 3 * strips + r * strips + strip
                        band[g, h, strip, pl.ds(r, triples, stride=3), :] = in_ref[pl.ds(at, triples, stride=per), :]
                    lanes = pl.ds((h * strips + strip) * LANES, LANES)
                    out_ref[g, :, lanes] = band[g, h, strip]

    return pl.pallas_call(
        body,
        out_shape=jax.ShapeDtypeStruct((n_ops, rows, width), F32),
        scratch_shapes=[pltpu.VMEM((n_ops, 2, strips, rows, LANES), F32)],
        cost_estimate=pl.CostEstimate(flops=0, bytes_accessed=8 * back.size, transcendentals=0),
        name="place_rows",
    )(back)


def coupling_matrix(slot_pair, sources, integrals, term_count):
    is_live = lax.broadcasted_iota(jnp.int32, sources.shape, 1) < term_count[:, None]
    weighted = jnp.where(is_live, integrals, jnp.zeros_like(integrals))
    matches = (sources[:, :, None] == slot_pair[None, None, :]).astype(F32)
    return jnp.sum(weighted[:, :, None] * matches, axis=1)


def by_slot(values, n_ops):
    rest = values.shape[1:]
    values = values.reshape(NX * NZ, NC, n_ops, *rest)
    return jnp.moveaxis(values, (2, 1, 0), (0, 1, 2)).reshape(-1, *rest)


def on_device(operators, rotations, sector_owner, slot_pair, sources, integrals, term_count):
    n_ops, _, _ = operators.shape
    y, c = lax.axis_index("y"), lax.axis_index("c")
    blocks = list(split_columns(operators, y[None]))
    for hop in range(1, NY):
        blocks[hop] = lax.ppermute(blocks[hop], "y", [(i, (i + hop) % NY) for i in range(NY)])
    coupling = coupling_matrix(*[by_slot(v, n_ops) for v in (slot_pair, sources, integrals, term_count)])
    own = spread_rotation(rotations[0], sector_owner[0])
    other = lax.ppermute(own, "c", [(0, 1), (1, 0)])
    width = rotations.shape[2]
    rows = width // NY
    left_done = multiply_left(jnp.stack([y, c]), own, blocks)
    left_done = multiply_left(jnp.stack([y, 1 - c]), other, blocks, left_done)
    by_row = exchange(left_done, "y")
    chunks = multiply_right(c[None], by_row, own, other)
    spread = exchange(chunks.reshape(N_PAIR, -1), ("c", "x", "z"))
    mixture = mix(coupling, spread.reshape(-1, LANES))
    back = exchange(mixture.reshape(N_PAIR, -1), ("c", "x", "z"))
    return place_rows(back.reshape(-1, LANES), rows, width)


def solution(mesh):
    torus = Mesh(mesh.devices.reshape(NX, NZ, NC, NY), ("x", "z", "c", "y"))

    in_specs = (P(PAIR, "y", None), P(PAIR, "y", None), P(), P(), P(), P(), P())
    return jax.shard_map(on_device, mesh=torus, in_specs=in_specs, out_specs=P(PAIR, "y", None), check_vma=False)
```

```python
import jax
import jax.numpy as jnp
from jax import lax
from jax.experimental import pallas as pl
from jax.experimental.pallas import tpu as pltpu
from jax.sharding import Mesh, PartitionSpec as P


NX, NZ, NC, NY = 4, 16, 2, 4
N_PAIR = NX * NZ * NC
PAIR = ("x", "z", "c")
LANES = 128
F32, BF16 = jnp.float32, jnp.bfloat16
VMEM = pl.BlockSpec(memory_space=pltpu.VMEM)
SMEM = pl.BlockSpec(memory_space=pltpu.SMEM)
GRANT = pltpu.CompilerParams(vmem_limit_bytes=12 << 20)


def exchange(chunks, axes):
    return lax.all_to_all(chunks, axes, split_axis=0, concat_axis=0, tiled=True)


def gather(piece, axes, count):
    return exchange(jnp.broadcast_to(piece, (count, *piece.shape)), axes)


def two_parts(value):
    high = value.astype(BF16)
    return high, (value - high.astype(F32)).astype(BF16)


def dot3(left, right, dims):
    (lh, ll), (rh, rl) = left, right

    def one(a, b):
        return lax.dot_general(a, b, (dims, ((), ())), preferred_element_type=F32)

    return one(lh, rh) + (one(lh, rl) + one(ll, rh))


def spread_rotation(slab, owner):
    x_own, z_own, c_own = owner // (NZ * NC), (owner // NC) % NZ, owner % NC
    flipped = slab.T
    new, few = flipped.shape
    rows = new // (NC * NX)
    piece = exchange(flipped.reshape(NC * NX, rows, few), ("c", "x"))
    piece = lax.dynamic_index_in_dim(piece, c_own * NX + x_own, 0, keepdims=False)
    piece = exchange(piece.reshape(NZ, rows // NZ, few), "z")
    piece = lax.dynamic_index_in_dim(piece, z_own, 0, keepdims=False)
    piece = gather(piece, "z", NZ).reshape(rows, few)
    piece = gather(piece, ("y", "x"), NY * NX)
    return piece.reshape(NY, NX * rows, few)


def split_columns(operators, y):
    n_ops, few, old = operators.shape
    cols = old // NY

    def body(y_ref, *refs):
        for source, target in zip(refs[:NY], refs[NY:], strict=True):
            target[...] = source[0]

    return pl.pallas_call(
        body,
        grid_spec=pltpu.PrefetchScalarGridSpec(
            num_scalar_prefetch=1,
            grid=(n_ops,),
            in_specs=[
                pl.BlockSpec((1, few, cols), lambda g, y_ref, hop=hop: (g, 0, lax.rem(y_ref[0] + hop, NY)))
                for hop in range(NY)
            ],
            out_specs=[pl.BlockSpec((few, cols), lambda g, y_ref: (0, g))] * NY,
        ),
        out_shape=[jax.ShapeDtypeStruct((few, n_ops * cols), F32)] * NY,
        cost_estimate=pl.CostEstimate(flops=0, bytes_accessed=8 * operators.size, transcendentals=0),
        compiler_params=GRANT,
        name="split_columns",
    )(y, *[operators] * NY)


def split_blocks(y, blocks):
    few, wide = blocks[0].shape

    def body(y_ref, *refs):
        high_ref, low_ref = refs[NY:]
        for hop in range(NY):
            at = pl.ds(pl.multiple_of(lax.rem(y_ref[0] + NY - hop, NY) * few, few), few)
            high_ref[at, :], low_ref[at, :] = two_parts(refs[hop][...])

    return pl.pallas_call(
        body,
        in_specs=[SMEM] + [VMEM] * NY,
        out_specs=[VMEM] * 2,
        out_shape=[jax.ShapeDtypeStruct((NY * few, wide), BF16)] * 2,
        cost_estimate=pl.CostEstimate(flops=0, bytes_accessed=32 * blocks[0].size, transcendentals=0),
        compiler_params=GRANT,
        name="split_blocks",
    )(y, *blocks)


def split_half(half, th, tl):
    for s in range(NY):
        at = pl.ds(s * half.shape[2], half.shape[2])
        th[:, at], tl[:, at] = two_parts(half[s])


def multiply_left(core, half, parts, first):
    n_half, depth = half.shape[1], parts[0].shape[0]
    wide = parts[0].shape[1]
    rows = n_half // 2
    both = first is not None

    def body(core_ref, half_ref, oh, ol, *refs):
        out, th, tl = refs[-3:]
        split_half(half_ref, th, tl)
        done = dot3((th[...], tl[...]), (oh[...], ol[...]), ((1,), (0,)))
        for q in range(2):
            if both:
                out[(1 - core_ref[0]) * 2 + q] = done[q * rows : (q + 1) * rows]
                out[core_ref[0] * 2 + q] = refs[0][q]
            else:
                out[q] = done[q * rows : (q + 1) * rows]

    return pl.pallas_call(
        body,
        in_specs=[SMEM] + [VMEM] * (4 if both else 3),
        out_specs=[VMEM] * 3,
        out_shape=[jax.ShapeDtypeStruct((4 if both else 2, rows, wide), F32)]
        + [jax.ShapeDtypeStruct((n_half, depth), BF16)] * 2,
        cost_estimate=pl.CostEstimate(
            flops=6 * n_half * depth * wide, bytes_accessed=4 * n_half * depth, transcendentals=0
        ),
        compiler_params=GRANT,
        name="multiply_left",
    )(core, half, *parts, *([first] if both else []))


def multiply_right(core, by_row, own, other):
    rows = by_row.shape[1]
    n_half, depth = own[0].shape
    few = depth // NY
    n_ops = by_row.shape[2] // few
    triples, strips = rows // 3, n_half // LANES
    per = n_ops * 3 * strips

    def body(core_ref, row_ref, *refs):
        pairs = refs[:2], refs[2:4]
        out_ref, rh, rl, z = refs[4:]
        for s in range(NY):
            at = pl.ds(s * few, few)
            for g in range(n_ops):
                band = pl.ds(g * rows, rows)
                rh[band, at], rl[band, at] = two_parts(row_ref[s, :, g * few : (g + 1) * few])
        for turn, (th, tl) in enumerate(pairs):
            done = dot3((rh[...], rl[...]), (th[...], tl[...]), ((1,), (1,)))
            side = core_ref[0] if turn == 0 else 1 - core_ref[0]
            for strip in range(strips):
                z[turn, strip] = done[:, strip * LANES : (strip + 1) * LANES]
            for g in range(n_ops):
                for r in range(3):
                    for strip in range(strips):
                        at = g * 3 * strips + r * strips + strip
                        out_ref[side, pl.ds(at, triples, stride=per), :] = z[
                            turn, strip, pl.ds(g * rows + r, triples, stride=3), :
                        ]

    out = (2, triples * per, LANES)
    return pl.pallas_call(
        body,
        in_specs=[SMEM] + [VMEM] * 5,
        out_specs=VMEM,
        out_shape=jax.ShapeDtypeStruct(out, F32),
        scratch_shapes=[
            pltpu.VMEM((n_ops * rows, depth), BF16),
            pltpu.VMEM((n_ops * rows, depth), BF16),
            pltpu.VMEM((2, strips, n_ops * rows, LANES), F32),
        ],
        cost_estimate=pl.CostEstimate(
            flops=12 * n_ops * rows * depth * n_half, bytes_accessed=8 * n_half * depth, transcendentals=0
        ),
        compiler_params=GRANT,
        name="multiply_right",
    )(core, by_row, *own, *other)


def mix(coupling, spread):
    n_all = coupling.shape[0]
    n_ops = n_all // N_PAIR
    per = spread.shape[0] // N_PAIR
    strips = per // n_ops

    def body(c_ref, x_ref, out_ref, xh, xl):
        for g in range(n_ops):
            for k in range(strips):
                part = x_ref[pl.ds(g * strips + k, N_PAIR, stride=per), :]
                at = (pl.ds(g * N_PAIR, N_PAIR), pl.ds(k * LANES, LANES))
                xh[at], xl[at] = two_parts(part)
        done = dot3(two_parts(c_ref[...]), (xh[...], xl[...]), ((1,), (0,)))
        for g in range(n_ops):
            for k in range(strips):
                out_ref[pl.ds(g * strips + k, N_PAIR, stride=per), :] = done[
                    g * N_PAIR : (g + 1) * N_PAIR, k * LANES : (k + 1) * LANES
                ]

    return pl.pallas_call(
        body,
        in_specs=[VMEM] * 2,
        out_specs=VMEM,
        out_shape=jax.ShapeDtypeStruct(spread.shape, F32),
        scratch_shapes=[pltpu.VMEM((n_all, strips * LANES), BF16)] * 2,
        cost_estimate=pl.CostEstimate(
            flops=6 * n_all * n_all * strips * LANES, bytes_accessed=8 * spread.size, transcendentals=0
        ),
        compiler_params=GRANT,
        name="mix",
    )(coupling, spread)


def place_rows(back, rows, width):
    triples = rows // 3
    strips = width // 2 // LANES
    per = back.shape[0] // (2 * triples)
    n_ops = per // (3 * strips)

    def body(in_ref, out_ref, band):
        for g in range(n_ops):
            for h in range(2):
                for strip in range(strips):
                    for r in range(3):
                        at = h * triples * per + g * 3 * strips + r * strips + strip
                        band[g, h, strip, pl.ds(r, triples, stride=3), :] = in_ref[pl.ds(at, triples, stride=per), :]
                    lanes = pl.ds((h * strips + strip) * LANES, LANES)
                    out_ref[g, :, lanes] = band[g, h, strip]

    return pl.pallas_call(
        body,
        in_specs=[VMEM],
        out_shape=jax.ShapeDtypeStruct((n_ops, rows, width), F32),
        scratch_shapes=[pltpu.VMEM((n_ops, 2, strips, rows, LANES), F32)],
        cost_estimate=pl.CostEstimate(flops=0, bytes_accessed=8 * back.size, transcendentals=0),
        compiler_params=GRANT,
        name="place_rows",
    )(back)


def coupling_matrix(slot_pair, sources, integrals, term_count):
    is_live = lax.broadcasted_iota(jnp.int32, sources.shape, 1) < term_count[:, None]
    weighted = jnp.where(is_live, integrals, jnp.zeros_like(integrals))
    matches = (sources[:, :, None] == slot_pair[None, None, :]).astype(F32)
    return jnp.sum(weighted[:, :, None] * matches, axis=1)


def by_slot(values, n_ops):
    rest = values.shape[1:]
    values = values.reshape(NX * NZ, NC, n_ops, *rest)
    return jnp.moveaxis(values, (2, 1, 0), (0, 1, 2)).reshape(-1, *rest)


def on_device(operators, rotations, sector_owner, slot_pair, sources, integrals, term_count):
    n_ops, _, _ = operators.shape
    y, c = lax.axis_index("y"), lax.axis_index("c")
    blocks = list(split_columns(operators, y[None]))
    for hop in range(1, NY):
        blocks[hop] = lax.ppermute(blocks[hop], "y", [(i, (i + hop) % NY) for i in range(NY)])
    coupling = coupling_matrix(*[by_slot(v, n_ops) for v in (slot_pair, sources, integrals, term_count)])
    parts = split_blocks(y[None], blocks)
    own = spread_rotation(rotations[0], sector_owner[0])
    other = lax.ppermute(own, "c", [(0, 1), (1, 0)])
    width = rotations.shape[2]
    rows = width // NY
    first, *own_parts = multiply_left(c[None], own, parts, None)
    left_done, *other_parts = multiply_left(c[None], other, parts, first)
    by_row = exchange(left_done, "y")
    chunks = multiply_right(c[None], by_row, own_parts, other_parts)
    spread = exchange(chunks.reshape(N_PAIR, -1), ("c", "x", "z"))
    mixture = mix(coupling, spread.reshape(-1, LANES))
    back = exchange(mixture.reshape(N_PAIR, -1), ("c", "x", "z"))
    return place_rows(back.reshape(-1, LANES), rows, width)


def solution(mesh):
    torus = Mesh(mesh.devices.reshape(NX, NZ, NC, NY), ("x", "z", "c", "y"))

    in_specs = (P(PAIR, "y", None), P(PAIR, "y", None), P(), P(), P(), P(), P())
    return jax.shard_map(on_device, mesh=torus, in_specs=in_specs, out_specs=P(PAIR, "y", None), check_vma=False)
```
